32 devices in a mesh: segment: 2 (over x), blk: 16 (over z, y, core).
Axes of the slice: x: 2, y: 2, z: 4, core: 2. Of those that a mesh axis runs over, the one named last changes fastest.
Arguments:
- pixels: bfloat16 [128, 4, 2048], P('segment', None, 'blk'), may hold values from -6 to 6
- var_group: int32 [128], P('segment'), may hold values from 0 to 7
- var_embed: bfloat16 [128, 2048], P('segment'), may hold values from -3 to 3
- group_weight: bfloat16 [8, 4, 2048], replicated, may hold values from -3 to 3
- agg_query: bfloat16 [2048], replicated, may hold values from -180 to 180
- lat_index: int32 [2048], P('blk'), may hold values from 0 to 359
- lat_table: bfloat16 [360, 2048], replicated, may hold values from -6 to 6
- norm_gain: float32 [2048], replicated, may hold values from 0.1 to 1.9
- w_query: bfloat16 [2048, 1024], P(None, 'segment'), may hold values from -9 to 9
- w_key: bfloat16 [2048, 1024], P(None, 'segment'), may hold values from -0.125 to 0.125
- w_value: bfloat16 [2048, 1024], P(None, 'segment'), may hold values from -0.125 to 0.125
- w_out: bfloat16 [1024, 2048], P('segment'), may hold values from -1.796875 to 1.796875
Outputs:
- aggregated: bfloat16 [2048, 2048], P('blk', 'segment')
- attended: bfloat16 [2048, 2048], P('blk', 'segment')
The draws below stay inside these ranges and needn't reach their ends.
All inputs are finite; a program needn't handle non-finite values.
Results may differ from the reference program's by a relative error of at most 0.015.
The reference program's roundings to bfloat16 on the way count: a program that leaves them out, or rounds other values in their place, can miss the bound.
Values may be sent and summed in bfloat16 or wider, within the bound.
A program may use at most 64 MiB of HBM per device.

```python
import math
import jax
import jax.numpy as jnp
from jax import lax

D = 2048
HEADS = 8
HEAD_DIM = 128
VARS = 128
PIX = 4
GROUPS = 8
NLAT = 360
TOKENS = 2048


def draw_agg_query(key, part):
    base = jnp.clip(jax.random.normal(key, (D,), jnp.float32), -3.0, 3.0)
    return base.astype(jnp.bfloat16)


def draw_w_query(key, part):
    columns = HEADS * HEAD_DIM
    base = jnp.clip(jax.random.normal(key, (D, columns), jnp.float32), -3.0, 3.0) * (2.0 / math.sqrt(D))
    return base.astype(jnp.bfloat16)


def set_ends(values, key, least, top_value):
    dims = values.shape
    index_at = [jax.random.randint(jax.random.fold_in(key, axis), (), 0, dims[axis]) for axis in range(len(dims))]
    values = values.at[tuple(index_at)].set(least)
    longest = dims.index(max(dims))
    index_at[longest] = (index_at[longest] + 1) % dims[longest]
    return values.at[tuple(index_at)].set(top_value)


def levels(own_key, shape, split, least, high):
    loudness, own = 1.0, jax.random.fold_in(own_key, 6)
    for dim, parts in split:
        heights = jnp.exp(jax.random.uniform(jax.random.fold_in(own, dim), (parts,), jnp.float32, least / len(split), high / len(split)))
        loudness = loudness * jnp.repeat(heights, shape[dim] // parts).reshape([-1 if axis == dim else 1 for axis in range(len(shape))])
    return loudness


def centred(stream_key, extent, scale, most, cuts=(), held_as=jnp.bfloat16):
    values = jax.random.normal(stream_key, extent, jnp.float32) * scale
    if len(cuts) > 0:
        values = levels(stream_key, extent, cuts, -0.22, 0.18) * values
    return jnp.clip(values, min=-most, max=most).astype(held_as)


def setup_inputs(seed: int = 0) -> dict:
    arg_keys = jax.random.split(jax.random.key(seed), 13)
    pixels = centred(arg_keys[0], (VARS, PIX, TOKENS), 1.0, 6.0, ((0, 2), (2, 16)))
    var_group = set_ends(jax.random.randint(arg_keys[1], (VARS,), 0, GROUPS), jax.random.fold_in(arg_keys[1], 1), 0, GROUPS - 1).astype(jnp.int32)
    var_embed = centred(arg_keys[2], (VARS, D), 0.5, 3.0, ((0, 2),))
    group_weight = centred(arg_keys[3], (GROUPS, PIX, D), PIX ** -0.5, 3.0)
    agg_query = draw_agg_query(jax.random.fold_in(arg_keys[12], 71), 0)
    lat_index = set_ends(jax.random.randint(arg_keys[5], (TOKENS,), 0, NLAT), jax.random.fold_in(arg_keys[5], 1), 0, NLAT - 1).astype(jnp.int32)
    lat_table = centred(arg_keys[6], (NLAT, D), 1.0, 6.0)
    norm_gain = jnp.clip(1.0 + 0.18 * jax.random.normal(arg_keys[7], (D,), jnp.float32), 0.1, 1.9)
    w_query = draw_w_query(jax.random.fold_in(arg_keys[12], 71), 0)
    w_key = centred(arg_keys[9], (D, HEADS * HEAD_DIM), D ** -0.5, 0.125, ((1, 2),))
    w_value = centred(arg_keys[10], (D, HEADS * HEAD_DIM), D ** -0.5, 0.125, ((1, 2),))
    w_out = centred(arg_keys[11], (HEADS * HEAD_DIM, D), 0.3, 1.796875, ((0, 2),))
    return dict(pixels=pixels, var_group=var_group, var_embed=var_embed, group_weight=group_weight, agg_query=agg_query, lat_index=lat_index, lat_table=lat_table, norm_gain=norm_gain, w_query=w_query, w_key=w_key, w_value=w_value, w_out=w_out)


def attend_head(stack):
    queries, keys, values = stack
    scale = 1.0 / math.sqrt(HEAD_DIM)
    qblock = math.gcd(TOKENS, 1024)
    blocks = queries.reshape(TOKENS // qblock, qblock, HEAD_DIM)

    def one_block(qrows):
        logits = jnp.dot(qrows, keys.T, precision=lax.Precision.HIGHEST) * scale
        peak = lax.optimization_barrier(jnp.max(logits, axis=1, keepdims=True))
        expo = jnp.exp(logits - peak)
        total = lax.optimization_barrier(jnp.sum(expo, axis=1, keepdims=True))
        rounded = lax.optimization_barrier(expo.astype(jnp.bfloat16))
        mixed = jnp.dot(rounded.astype(jnp.float32), values, precision=lax.Precision.HIGHEST)
        return mixed / total
    return lax.map(one_block, blocks).reshape(TOKENS, HEAD_DIM)

def reference(pixels, var_group, var_embed, group_weight, agg_query, lat_index, lat_table, norm_gain, w_query, w_key, w_value, w_out):
    highest = lax.Precision.HIGHEST
    query32 = agg_query.astype(jnp.float32)
    group32 = group_weight.astype(jnp.float32)
    embed32 = var_embed.astype(jnp.float32)
    pixel32 = pixels.astype(jnp.float32)
    proj_group = jnp.einsum('gpd,d->gp', group32, query32, precision=highest)
    onehot = (var_group[:, None] == jnp.arange(GROUPS, dtype=jnp.int32)[None, :]).astype(jnp.float32)
    proj_var = jnp.dot(onehot, proj_group, precision=highest)
    offset = jnp.dot(embed32, query32, precision=highest)
    scores = (jnp.einsum('vpt,vp->vt', pixel32, proj_var, precision=highest) + offset[:, None]) / math.sqrt(D)
    peak = lax.optimization_barrier(jnp.max(scores, axis=0))
    expo = jnp.exp(scores - peak[None, :])
    total = lax.optimization_barrier(jnp.sum(expo, axis=0))
    grouped = jnp.einsum('vg,vpt->gpt', onehot, expo[:, None, :] * pixel32, precision=highest)
    summed = jnp.einsum('vt,vd->td', expo, embed32, precision=highest)
    summed = summed + jnp.einsum('gpt,gpd->td', grouped, group32, precision=highest)
    latent = summed / total[:, None] + jnp.take(lat_table, lat_index, axis=0).astype(jnp.float32)
    center = latent - lax.optimization_barrier(jnp.mean(latent, axis=1, keepdims=True))
    spread = lax.optimization_barrier(jnp.mean(center * center, axis=1, keepdims=True))
    normed = (center * lax.rsqrt(spread + 1e-05) * norm_gain[None, :]).astype(jnp.bfloat16)
    queries = jnp.dot(normed, w_query, preferred_element_type=jnp.float32).astype(jnp.bfloat16)
    keys = jnp.dot(normed, w_key, preferred_element_type=jnp.float32).astype(jnp.bfloat16)
    values = jnp.dot(normed, w_value, preferred_element_type=jnp.float32).astype(jnp.bfloat16)

    def split_heads(array):
        return array.astype(jnp.float32).reshape(TOKENS, HEADS, HEAD_DIM).transpose(1, 0, 2)
    heads = lax.map(attend_head, (split_heads(queries), split_heads(keys), split_heads(values)))
    heads_out = heads.transpose(1, 0, 2).reshape(TOKENS, HEADS * HEAD_DIM).astype(jnp.bfloat16)
    attended = jnp.dot(heads_out, w_out, preferred_element_type=jnp.float32).astype(jnp.bfloat16)
    return (latent.astype(jnp.bfloat16), attended)
```

```python
import functools
import math

import jax
import jax.numpy as jnp
from jax import lax
from jax.experimental import pallas as pl
from jax.experimental.pallas import tpu as pltpu
from jax.sharding import PartitionSpec as P

HEAD_DIM = 128
MESH = pl.DeviceIdType.MESH
F32 = jnp.float32
BF16 = jnp.bfloat16


def kernel(
    S, R, C,
    pix_ref, vg_ref, emb_ref, gw_ref, q_ref, lidx_ref, lat_ref, gain_ref,
    wq_ref, wk_ref, wv_ref, wo_ref,
    agg_ref, att_ref,
    bm, latv, wqv, wkv, wvv, woa, gtmp, pixf, cf, ck, lt, nm, kv, qs, ms, ls, acc, ho,
    loc, e_s, e_r, ep_s, ep_r, c_s, c_r, o_s, o_r, op_s, op_r, h_s, h_r, k_s, k_r,
):
    D = emb_ref.shape[1]
    Vl = emb_ref.shape[0]
    G, PX, _ = gw_ref.shape
    GP = G * PX
    T = pix_ref.shape[2]
    NL = lat_ref.shape[0]
    Cl = wq_ref.shape[1]
    H = Cl // HEAD_DIM
    share = D // S
    half = D // 2
    clh = Cl // 2
    Kp = ck.shape[0]
    W = C * 2 * T
    s = lax.axis_index("segment")
    b = lax.axis_index("blk")
    c = lax.rem(b, 2)
    rc = b // 2
    col = lax.rem(rc, C)
    r = rc // C
    partner = b + 1 - 2 * c

    def dev(seg, blk):
        return {"segment": seg, "blk": blk}

    barrier = pltpu.get_barrier_semaphore()

    def greet(seg, blk):
        pl.semaphore_signal(barrier, inc=1, device_id=dev(seg, blk), device_id_type=MESH)

    for k in range(1, S):
        greet(lax.rem(s + k, S), b)
    greet(s, partner)
    pl.when(r > 0)(lambda: greet(s, b - 2 * C))
    pl.when(r < R - 1)(lambda: greet(s, b + 2 * C))
    pl.when(col > 0)(lambda: greet(s, b - 2))
    pl.when(col < C - 1)(lambda: greet(s, b + 2))

    own_rows = pl.ds(pl.multiple_of(s * Vl, Vl), Vl)
    locals_ = [
        pltpu.make_async_copy(emb_ref, bm.at[own_rows], loc.at[0]),
        pltpu.make_async_copy(lat_ref, latv, loc.at[1]),
        pltpu.make_async_copy(wk_ref, wkv, loc.at[2]),
        pltpu.make_async_copy(wv_ref, wvv, loc.at[3]),
        pltpu.make_async_copy(wq_ref, wqv, loc.at[4]),
        pltpu.make_async_copy(
            wo_ref.at[:, pl.ds(pl.multiple_of(s * share, share), share)], woa.at[s], loc.at[5]
        ),
    ]
    for one in locals_:
        one.start()
    count = (
        S
        + jnp.minimum(r, 1)
        + jnp.minimum(R - 1 - r, 1)
        + jnp.minimum(col, 1)
        + jnp.minimum(C - 1 - col, 1)
    )
    pl.semaphore_wait(barrier, count)

    def remote(src, dst, send, recv, seg, blk):
        return pltpu.make_async_remote_copy(
            src_ref=src, dst_ref=dst, send_sem=send, recv_sem=recv,
            device_id=dev(seg, blk), device_id_type=MESH,
        )

    def seg_at(k):
        return lax.rem(s + k, S)

    def emb_region(seg, core):
        return bm.at[
            pl.ds(pl.multiple_of(seg * Vl, Vl), Vl), pl.ds(pl.multiple_of(core * half, half), half)
        ]

    my_half = pl.ds(pl.multiple_of(c * half, half), half)
    e_out = [
        remote(emb_ref.at[:, my_half], emb_region(s, c), e_s.at[k], e_r.at[k], seg_at(k), b)
        for k in range(1, S)
    ]
    for one in e_out:
        one.start()

    q = q_ref[...]
    for g in range(G):
        one_group = gw_ref[g].astype(F32)
        for p in range(PX):
            gtmp[p * G + g : p * G + g + 1, :] = one_group[p : p + 1, :]
    gwp = gtmp[...]
    bm[S * Vl : S * Vl + GP, :] = gwp.astype(BF16)
    if Kp > S * Vl + GP:
        bm[S * Vl + GP : Kp, :] = jnp.zeros((Kp - S * Vl - GP, D), BF16)
    pg = jnp.sum(gwp * q, axis=1, keepdims=True)
    for v in range(Vl):
        pixf[PX * v : PX * v + PX, :] = pix_ref[v].astype(F32)
    vg = vg_ref[...]
    row_at = lax.broadcasted_iota(jnp.int32, (Vl, Vl), 0)
    col_at = lax.broadcasted_iota(jnp.int32, (Vl, Vl), 1)
    vcol = jnp.sum(jnp.where(row_at == col_at, vg.astype(F32), 0.0), axis=1, keepdims=True)
    onehot = (lax.broadcasted_iota(jnp.int32, (G, Vl), 0) == vg).astype(F32)
    locals_[0].wait()
    scores = jnp.sum(bm[own_rows, :].astype(F32) * q, axis=1, keepdims=True)
    planes = [pixf[pl.ds(p, Vl, stride=PX), :] for p in range(PX)]
    for p in range(PX):
        pv = jnp.zeros((Vl, 1), F32)
        for g in range(G):
            pv = jnp.where(vcol == float(g), pg[p * G + g : p * G + g + 1, :], pv)
        scores = scores + planes[p] * pv
    scores = scores / math.sqrt(D)
    peak = jnp.max(scores, axis=0, keepdims=True)
    expo = jnp.exp(scores - peak)
    cf[s, 0:Vl, :] = expo
    for p in range(PX):
        cf[s, Vl + p * G : Vl + p * G + G, :] = jnp.dot(
            onehot, expo * planes[p], precision=lax.Precision.HIGHEST, preferred_element_type=F32
        )
    top = Vl + GP
    cf[s, top : top + 8, :] = jnp.broadcast_to(peak, (8, T))
    cf[s, top + 8 : top + 16, :] = jnp.broadcast_to(jnp.sum(expo, axis=0, keepdims=True), (8, T))
    c_out = [
        remote(cf.at[s], cf.at[s], c_s.at[k], c_r.at[k], seg_at(k), b) for k in range(1, S)
    ]
    for one in c_out:
        one.start()

    def wo_rows(core):
        return pl.ds(pl.multiple_of(core * clh, clh), clh)

    o_out = [
        remote(
            wo_ref.at[wo_rows(c), pl.ds(pl.multiple_of(seg_at(k) * share, share), share)],
            woa.at[s, wo_rows(c)], o_s.at[k], o_r.at[k], seg_at(k), b,
        )
        for k in range(1, S)
    ]
    for one in o_out:
        one.start()

    lat_rows = ((NL + 127) // 128) * 128
    hot = (lax.broadcasted_iota(jnp.int32, (lat_rows, T), 0) == lidx_ref[...]).astype(F32)
    hot = hot.T.astype(BF16)[:, :NL]

    ep_out = []
    for k in range(1, S):
        src = seg_at(S - k)
        remote(emb_region(src, c), emb_region(src, c), e_s.at[k], e_r.at[k], s, partner).wait_recv()
        one = remote(
            emb_region(src, c), emb_region(src, c), ep_s.at[k], ep_r.at[k], s, partner
        )
        one.start()
        ep_out.append(one)
    for k in range(1, S):
        src = seg_at(S - k)
        remote(cf.at[src], cf.at[src], c_s.at[k], c_r.at[k], s, partner).wait_recv()
    best = cf[0, top : top + 1, :]
    for k in range(1, S):
        best = jnp.maximum(best, cf[k, top : top + 1, :])
    factors = [jnp.exp(cf[k, top : top + 1, :] - best) for k in range(S)]
    total = factors[0] * cf[0, top + 8 : top + 9, :]
    for k in range(1, S):
        total = total + factors[k] * cf[k, top + 8 : top + 9, :]
    grouped = jnp.zeros((GP, T), F32)
    for k in range(S):
        share_k = factors[k] / total
        ck[k * Vl : k * Vl + Vl, :] = cf[k, 0:Vl, :] * share_k
        grouped = grouped + cf[k, Vl : Vl + GP, :] * share_k
    ck[S * Vl : S * Vl + GP, :] = grouped
    if Kp > S * Vl + GP:
        ck[S * Vl + GP : Kp, :] = jnp.zeros((Kp - S * Vl - GP, T), F32)
    ct = ck[...].T
    hi = ct.astype(BF16)
    rest = ct - hi.astype(F32)
    mid = rest.astype(BF16)
    low = (rest - mid.astype(F32)).astype(BF16)
    for k in range(1, S):
        src = seg_at(S - k)
        other = emb_region(src, 1 - c)
        remote(other, other, ep_s.at[k], ep_r.at[k], s, partner).wait_recv()
    locals_[1].wait()
    step = 512
    mean = jnp.zeros((T, 1), F32)
    for j in range(D // step):
        at = slice(j * step, (j + 1) * step)
        base = bm[:, at]
        part = jnp.dot(low, base, preferred_element_type=F32)
        part = part + jnp.dot(mid, base, preferred_element_type=F32)
        part = part + jnp.dot(hi, base, preferred_element_type=F32)
        part = part + jnp.dot(hot, latv[:, at], preferred_element_type=F32)
        lt[:, at] = part
        mean = mean + jnp.sum(part, axis=1, keepdims=True)
    mean = mean / D
    spread = jnp.zeros((T, 1), F32)
    for j in range(D // step):
        center = lt[:, j * step : (j + 1) * step] - mean
        spread = spread + jnp.sum(center * center, axis=1, keepdims=True)
    inv = lax.rsqrt(spread / D + 1e-05)
    for j in range(D // step):
        at = slice(j * step, (j + 1) * step)
        nm[:, at] = ((lt[:, at] - mean) * inv * gain_ref[:, at]).astype(BF16)

    def region(part, blk):
        return kv.at[part, pl.ds(pl.multiple_of(blk * T, T), T)]

    def sends(r0, c0, act):
        blk = (r0 * C + c0) * 2 + c
        here = c0 == col

        def each(part, way, to):
            return remote(
                region(part, blk), region(part, blk), k_s.at[way, part, blk], k_r.at[part, blk],
                s, to,
            )

        def go(part):
            pl.when(here & (r > 0) & (r0 >= r))(lambda: act(each(part, 0, b - 2 * C)))
            pl.when(here & (r < R - 1) & (r0 <= r))(lambda: act(each(part, 1, b + 2 * C)))
            pl.when((col > 0) & (c0 >= col))(lambda: act(each(part, 2, b - 2)))
            pl.when((col < C - 1) & (c0 <= col))(lambda: act(each(part, 3, b + 2)))
            act(each(part, 4, partner))

        return go

    def start(copy):
        copy.start()

    def arrived(part, blk):
        remote(
            region(part, blk), region(part, blk), k_s.at[4, part, blk], k_r.at[part, blk],
            s, partner,
        ).wait_recv()

    mine = sends(r, col, start)
    own_keys = pl.ds(pl.multiple_of(b * T, T), T)
    locals_[2].wait()
    kv[0, own_keys, :] = jnp.dot(nm[...], wkv[...], preferred_element_type=F32).astype(BF16)
    mine(0)
    locals_[3].wait()
    kv[1, own_keys, :] = jnp.dot(nm[...], wvv[...], preferred_element_type=F32).astype(BF16)
    mine(1)
    locals_[4].wait()
    qs[...] = jnp.dot(nm[...], wqv[...], preferred_element_type=F32).astype(BF16)
    agg_ref[...] = lt[:, pl.ds(pl.multiple_of(s * share, share), share)].astype(BF16)
    ms[...] = jnp.full(ms.shape, -1e30, F32)
    ls[...] = jnp.zeros(ls.shape, F32)
    acc[...] = jnp.zeros(acc.shape, F32)
    scale = 1.0 / math.sqrt(HEAD_DIM)

    def attend(row):
        keys_at = pl.ds(pl.multiple_of(row * W, W), W)
        for h in range(H):
            cols = slice(h * HEAD_DIM, (h + 1) * HEAD_DIM)
            logits = (
                lax.dot_general(
                    qs[:, cols], kv[0, keys_at, cols], (((1,), (1,)), ((), ())),
                    preferred_element_type=F32,
                )
                * scale
            )
            old = ms[h]
            fresh = jnp.maximum(old, jnp.max(logits, axis=1, keepdims=True))
            shrink = jnp.exp(old - fresh)
            expo = jnp.exp(logits - fresh[:, 0:1])
            ls[h] = ls[h] * shrink + jnp.sum(expo, axis=1, keepdims=True)
            ms[h] = fresh
            acc[:, cols] = acc[:, cols] * shrink[:, 0:1] + jnp.dot(
                expo.astype(BF16), kv[1, keys_at, cols], preferred_element_type=F32
            )

    def from_column(row):
        for part in range(2):
            arrived(part, (row * C + col) * 2 + c)
            sends(row, col, start)(part)

    def finish(row):
        for dist in range(1, C):
            for way in (-1, 1):
                c0 = col + way * dist

                @pl.when((c0 >= 0) & (c0 < C))
                def _():
                    for part in range(2):
                        arrived(part, (row * C + c0) * 2 + c)
                        sends(row, c0, start)(part)

        for c0 in range(C):
            for part in range(2):
                arrived(part, (row * C + c0) * 2 + 1 - c)
        attend(row)

    def stage(d, carry):
        def ahead(way, inner):
            row = r + (2 * way - 1) * (d + 1)
            pl.when((row >= 0) & (row < R))(lambda: from_column(row))
            return inner

        lax.fori_loop(0, 2, ahead, 0)

        def now(way, inner):
            row = r + (2 * way - 1) * d
            pl.when((row >= 0) & (row < R) & (d + way > 0))(lambda: finish(row))
            return inner

        lax.fori_loop(0, 2, now, 0)
        return carry

    lax.fori_loop(0, R, stage, 0)

    for h in range(H):
        cols = slice(h * HEAD_DIM, (h + 1) * HEAD_DIM)
        ho[s, :, cols] = (acc[:, cols] / ls[h][:, 0:1]).astype(BF16)
    h_out = [remote(ho.at[s], ho.at[s], h_s.at[k], h_r.at[k], seg_at(k), b) for k in range(1, S)]
    for one in h_out:
        one.start()
    op_out = []
    for k in range(1, S):
        src = seg_at(S - k)
        block = woa.at[src, wo_rows(c)]
        remote(block, block, o_s.at[k], o_r.at[k], s, partner).wait_recv()
        one = remote(block, block, op_s.at[k], op_r.at[k], s, partner)
        one.start()
        op_out.append(one)
    locals_[5].wait()
    lt[:, 0:share] = jnp.dot(ho[s], woa[s], preferred_element_type=F32)
    for k in range(1, S):
        src = seg_at(S - k)
        block = woa.at[src, wo_rows(1 - c)]
        remote(block, block, op_s.at[k], op_r.at[k], s, partner).wait_recv()
        remote(ho.at[src], ho.at[src], h_s.at[k], h_r.at[k], s, partner).wait_recv()
        lt[:, 0:share] = lt[:, 0:share] + jnp.dot(ho[src], woa[src], preferred_element_type=F32)
    att_ref[...] = lt[:, 0:share].astype(BF16)

    for one in e_out + ep_out + c_out + o_out + op_out + h_out:
        one.wait_send()

    def drain(i, carry):
        ends = sends(i // C, lax.rem(i, C), lambda copy: copy.wait_send())
        ends(0)
        ends(1)
        return carry

    lax.fori_loop(0, R * C, drain, 0)


def solution(mesh):
    S = mesh.shape["segment"]
    B = mesh.shape["blk"]
    chips = B // 2
    C = 1
    while C * C * 4 <= chips:
        C *= 2
    R = chips // C

    def on_device(
        pixels, var_group, var_embed, group_weight, agg_query, lat_index, lat_table, norm_gain,
        w_query, w_key, w_value, w_out,
    ):
        vl, D = var_embed.shape
        G, PX, _ = group_weight.shape
        T = pixels.shape[2]
        NL = lat_table.shape[0]
        cl = w_query.shape[1]
        H = cl // HEAD_DIM
        share = D // S
        kp = ((S * vl + G * PX + 127) // 128) * 128
        vm = pl.BlockSpec(memory_space=pltpu.VMEM)
        far = pl.BlockSpec(memory_space=pl.ANY)
        dma = pltpu.SemaphoreType.DMA
        out = jax.ShapeDtypeStruct((T, share), BF16)
        return pl.pallas_call(
            functools.partial(kernel, S, R, C),
            out_shape=(out, out),
            in_specs=[vm, vm, far, vm, vm, vm, far, vm, far, far, far, far],
            out_specs=(vm, vm),
            scratch_shapes=[
                pltpu.VMEM((kp, D), BF16),
                pltpu.VMEM((NL, D), BF16),
                pltpu.VMEM((D, cl), BF16),
                pltpu.VMEM((D, cl), BF16),
                pltpu.VMEM((D, cl), BF16),
                pltpu.VMEM((S, cl, share), BF16),
                pltpu.VMEM((G * PX, D), F32),
                pltpu.VMEM((vl * PX, T), F32),
                pltpu.VMEM((S, vl + G * PX + 16, T), F32),
                pltpu.VMEM((kp, T), F32),
                pltpu.VMEM((T, D), F32),
                pltpu.VMEM((T, D), BF16),
                pltpu.VMEM((2, B * T, cl), BF16),
                pltpu.VMEM((T, cl), BF16),
                pltpu.VMEM((H, T, 128), F32),
                pltpu.VMEM((H, T, 128), F32),
                pltpu.VMEM((T, cl), F32),
                pltpu.VMEM((S, T, cl), BF16),
                dma((6,)),
            ]
            + [dma((S,))] * 12
            + [dma((5, 2, B)), dma((2, B))],
            compiler_params=pltpu.CompilerParams(
                collective_id=0, has_side_effects=True, vmem_limit_bytes=48 * 1024 * 1024
            ),
        )(
            pixels,
            var_group.reshape(1, vl),
            var_embed,
            group_weight,
            agg_query.astype(F32).reshape(1, D),
            lat_index.reshape(1, T),
            lat_table,
            norm_gain.reshape(1, D),
            w_query,
            w_key,
            w_value,
            w_out,
        )

    in_specs = (
        P("segment", None, "blk"), P("segment"), P("segment", None), P(), P(), P("blk"), P(), P(),
        P(None, "segment"), P(None, "segment"), P(None, "segment"), P("segment", None),
    )
    out_specs = (P("blk", "segment"), P("blk", "segment"))
    return jax.shard_map(
        on_device, mesh=mesh, in_specs=in_specs, out_specs=out_specs, check_vma=False
    )
```

```python
import functools
import math

import jax
import jax.numpy as jnp
from jax import lax
from jax.experimental import pallas as pl
from jax.experimental.pallas import tpu as pltpu
from jax.sharding import PartitionSpec as P

HEAD_DIM = 128
MESH = pl.DeviceIdType.MESH
F32 = jnp.float32
BF16 = jnp.bfloat16


def kernel(
    S, R, C,
    pix_hbm, vg_hbm, emb_ref, gw_hbm, q_hbm, lidx_hbm, lat_ref, gain_hbm,
    wq_ref, wk_ref, wv_ref, wo_ref,
    agg_ref, att_ref,
    pix_ref, vg_ref, gw_ref, q_ref, lidx_ref, gain_ref,
    bm, latv, wqv, wkv, wvv, woa, gtmp, pixf, cf, ck, lt, nm, kv, qs, ms, ls, acc, ho,
    loc, e_s, e_r, ep_s, ep_r, c_s, c_r, o_s, o_r, op_s, op_r, h_s, h_r, y_s, y_r, k_s, k_r,
):
    D = emb_ref.shape[1]
    Vl = emb_ref.shape[0]
    G, PX, _ = gw_ref.shape
    GP = G * PX
    T = pix_ref.shape[2]
    NL = lat_ref.shape[0]
    Cl = wq_ref.shape[1]
    H = Cl // HEAD_DIM
    share = D // S
    half = D // 2
    clh = Cl // 2
    Kp = ck.shape[1]
    used = S * Vl + GP
    W = C * 2 * T
    s = lax.axis_index("segment")
    b = lax.axis_index("blk")
    c = lax.rem(b, 2)
    rc = b // 2
    col = lax.rem(rc, C)
    r = rc // C
    partner = b + 1 - 2 * c

    def dev(seg, blk):
        return {"segment": seg, "blk": blk}

    barrier = pltpu.get_barrier_semaphore()

    def greet(seg, blk):
        pl.semaphore_signal(barrier, inc=1, device_id=dev(seg, blk), device_id_type=MESH)

    for k in range(1, S):
        greet(lax.rem(s + k, S), b)
    greet(s, partner)
    pl.when(r > 0)(lambda: greet(s, b - 2 * C))
    pl.when(r < R - 1)(lambda: greet(s, b + 2 * C))
    for k in range(1, C):
        greet(s, b + 2 * (lax.rem(col + k, C) - col))

    own_rows = pl.ds(pl.multiple_of(s * Vl, Vl), Vl)
    small = [
        pltpu.make_async_copy(src, dst, loc.at[6 + i])
        for i, (src, dst) in enumerate(
            [(gw_hbm, gw_ref), (q_hbm, q_ref), (pix_hbm, pix_ref), (vg_hbm, vg_ref),
             (lidx_hbm, lidx_ref), (gain_hbm, gain_ref)]
        )
    ]
    for one in small[:2]:
        one.start()
    locals_ = [
        pltpu.make_async_copy(emb_ref, bm.at[own_rows], loc.at[0]),
        pltpu.make_async_copy(lat_ref, latv, loc.at[1]),
        pltpu.make_async_copy(wk_ref, wkv, loc.at[2]),
        pltpu.make_async_copy(wv_ref, wvv, loc.at[3]),
        pltpu.make_async_copy(wq_ref, wqv, loc.at[4]),
        pltpu.make_async_copy(
            wo_ref.at[:, pl.ds(pl.multiple_of(s * share, share), share)], woa.at[s], loc.at[5]
        ),
    ]
    locals_[0].start()
    for one in small[2:] + locals_[1:]:
        one.start()
    count = (
        S
        + C
        - 1
        + jnp.minimum(r, 1)
        + jnp.minimum(R - 1 - r, 1)
    )
    pl.semaphore_wait(barrier, count)

    def remote(src, dst, send, recv, seg, blk):
        return pltpu.make_async_remote_copy(
            src_ref=src, dst_ref=dst, send_sem=send, recv_sem=recv,
            device_id=dev(seg, blk), device_id_type=MESH,
        )

    def seg_at(k):
        return lax.rem(s + k, S)

    def emb_region(seg, core):
        return bm.at[
            pl.ds(pl.multiple_of(seg * Vl, Vl), Vl), pl.ds(pl.multiple_of(core * half, half), half)
        ]

    my_half = pl.ds(pl.multiple_of(c * half, half), half)
    e_out = [
        remote(emb_ref.at[:, my_half], emb_region(s, c), e_s.at[k], e_r.at[k], seg_at(k), b)
        for k in range(1, S)
    ]
    for one in e_out:
        one.start()

    small[1].wait()
    q = q_ref[...]
    small[0].wait()
    for g in range(G):
        one_group = gw_ref[g].astype(F32)
        for p in range(PX):
            gtmp[p * G + g : p * G + g + 1, :] = one_group[p : p + 1, :]
    gwp = gtmp[...]
    bm[S * Vl : S * Vl + GP, :] = gwp.astype(BF16)
    if Kp > S * Vl + GP:
        bm[S * Vl + GP : Kp, :] = jnp.zeros((Kp - S * Vl - GP, D), BF16)
    pg = jnp.sum(gwp * q, axis=1, keepdims=True)
    small[2].wait()
    for v in range(Vl):
        pixf[PX * v : PX * v + PX, :] = pix_ref[v].astype(F32)
    small[3].wait()
    vg = vg_ref[...]
    row_at = lax.broadcasted_iota(jnp.int32, (Vl, Vl), 0)
    col_at = lax.broadcasted_iota(jnp.int32, (Vl, Vl), 1)
    vcol = jnp.sum(jnp.where(row_at == col_at, vg.astype(F32), 0.0), axis=1, keepdims=True)
    onehot = (lax.broadcasted_iota(jnp.int32, (G, Vl), 0) == vg).astype(F32)
    locals_[0].wait()
    scores = jnp.sum(bm[own_rows, :].astype(F32) * q, axis=1, keepdims=True)
    planes = [pixf[pl.ds(p, Vl, stride=PX), :] for p in range(PX)]
    for p in range(PX):
        pv = jnp.zeros((Vl, 1), F32)
        for g in range(G):
            pv = jnp.where(vcol == float(g), pg[p * G + g : p * G + g + 1, :], pv)
        scores = scores + planes[p] * pv
    scores = scores / math.sqrt(D)
    peak = jnp.max(scores, axis=0, keepdims=True)
    expo = jnp.exp(scores - peak)
    cf[s, 0:Vl, :] = expo
    for p in range(PX):
        cf[s, Vl + p * G : Vl + p * G + G, :] = jnp.dot(
            onehot, expo * planes[p], precision=lax.Precision.HIGHEST, preferred_element_type=F32
        )
    top = Vl + GP
    cf[s, top : top + 8, :] = jnp.broadcast_to(peak, (8, T))
    cf[s, top + 8 : top + 16, :] = jnp.broadcast_to(jnp.sum(expo, axis=0, keepdims=True), (8, T))
    c_out = [
        remote(cf.at[s], cf.at[s], c_s.at[k], c_r.at[k], seg_at(k), b) for k in range(1, S)
    ]
    for one in c_out:
        one.start()

    def wo_rows(core):
        return pl.ds(pl.multiple_of(core * clh, clh), clh)

    o_out = [
        remote(
            wo_ref.at[wo_rows(c), pl.ds(pl.multiple_of(seg_at(k) * share, share), share)],
            woa.at[s, wo_rows(c)], o_s.at[k], o_r.at[k], seg_at(k), b,
        )
        for k in range(1, S)
    ]
    for one in o_out:
        one.start()

    small[4].wait()
    ck[col, used : used + 8, :] = jnp.broadcast_to(lidx_ref[...].astype(F32), (8, T))
    if Kp > used + 8:
        for c0 in range(C):
            ck[c0, used + 8 : Kp, :] = jnp.zeros((Kp - used - 8, T), F32)

    ep_out = []
    for k in range(1, S):
        src = seg_at(S - k)
        remote(emb_region(src, c), emb_region(src, c), e_s.at[k], e_r.at[k], s, partner).wait_recv()
        one = remote(
            emb_region(src, c), emb_region(src, c), ep_s.at[k], ep_r.at[k], s, partner
        )
        one.start()
        ep_out.append(one)
    for k in range(1, S):
        src = seg_at(S - k)
        remote(cf.at[src], cf.at[src], c_s.at[k], c_r.at[k], s, partner).wait_recv()
    best = cf[0, top : top + 1, :]
    for k in range(1, S):
        best = jnp.maximum(best, cf[k, top : top + 1, :])
    factors = [jnp.exp(cf[k, top : top + 1, :] - best) for k in range(S)]
    total = factors[0] * cf[0, top + 8 : top + 9, :]
    for k in range(1, S):
        total = total + factors[k] * cf[k, top + 8 : top + 9, :]
    grouped = jnp.zeros((GP, T), F32)
    for k in range(S):
        share_k = factors[k] / total
        ck[col, k * Vl : k * Vl + Vl, :] = cf[k, 0:Vl, :] * share_k
        grouped = grouped + cf[k, Vl : Vl + GP, :] * share_k
    ck[col, S * Vl : used, :] = grouped
    y_out = []
    for k in range(1, C):
        to = lax.rem(col + k, C)
        block = ck.at[col, pl.ds(0, used + 8)]
        one = remote(block, block, y_s.at[k], y_r.at[k], s, b + 2 * (to - col))
        one.start()
        y_out.append(one)
    small[5].wait()

    def region(part, blk):
        return kv.at[part, pl.ds(pl.multiple_of(blk * T, T), T)]

    def sends(r0, c0, act):
        blk = (r0 * C + c0) * 2 + c
        here = c0 == col

        def each(part, way, to):
            return remote(
                region(part, blk), region(part, blk), k_s.at[way, part, blk], k_r.at[part, blk],
                s, to,
            )

        def go(part):
            pl.when(here & (r > 0) & (r0 >= r))(lambda: act(each(part, 0, b - 2 * C)))
            pl.when(here & (r < R - 1) & (r0 <= r))(lambda: act(each(part, 1, b + 2 * C)))
            pl.when((r0 != r) & (col > 0) & (c0 >= col))(lambda: act(each(part, 2, b - 2)))
            pl.when((r0 != r) & (col < C - 1) & (c0 <= col))(lambda: act(each(part, 3, b + 2)))
            act(each(part, 4, partner))

        return go

    def start(copy):
        copy.start()

    def arrived(part, blk):
        remote(
            region(part, blk), region(part, blk), k_s.at[4, part, blk], k_r.at[part, blk],
            s, partner,
        ).wait_recv()

    lat_rows = ((NL + 127) // 128) * 128
    step = 512

    def own_block(turn, carry):
        c0 = lax.rem(col + turn, C)

        @pl.when(turn > 0)
        def _():
            block = ck.at[c0, pl.ds(0, used + 8)]
            back = C - turn
            remote(block, block, y_s.at[back], y_r.at[back], s, partner).wait_recv()

        ct = ck[c0].T
        hi = ct.astype(BF16)
        rest = ct - hi.astype(F32)
        mid = rest.astype(BF16)
        low = (rest - mid.astype(F32)).astype(BF16)
        at_row = ck[c0, used : used + 1, :]
        rows = lax.broadcasted_iota(jnp.int32, (lat_rows, T), 0).astype(F32)
        hot = (rows == at_row).astype(F32).T.astype(BF16)[:, :NL]

        @pl.when(turn == 0)
        def _():
            for k in range(1, S):
                other = emb_region(seg_at(S - k), 1 - c)
                remote(other, other, ep_s.at[k], ep_r.at[k], s, partner).wait_recv()
            locals_[1].wait()

        mean = jnp.zeros((T, 1), F32)
        for j in range(D // step):
            at = slice(j * step, (j + 1) * step)
            base = bm[:, at]
            part = jnp.dot(low, base, preferred_element_type=F32)
            part = part + jnp.dot(mid, base, preferred_element_type=F32)
            part = part + jnp.dot(hi, base, preferred_element_type=F32)
            part = part + jnp.dot(hot, latv[:, at], preferred_element_type=F32)
            lt[:, at] = part
            mean = mean + jnp.sum(part, axis=1, keepdims=True)
        mean = mean / D
        spread = jnp.zeros((T, 1), F32)
        for j in range(D // step):
            center = lt[:, j * step : (j + 1) * step] - mean
            spread = spread + jnp.sum(center * center, axis=1, keepdims=True)
        inv = lax.rsqrt(spread / D + 1e-05)
        for j in range(D // step):
            at = slice(j * step, (j + 1) * step)
            nm[:, at] = ((lt[:, at] - mean) * inv * gain_ref[:, at]).astype(BF16)

        blk = (r * C + c0) * 2 + c
        keys_at = pl.ds(pl.multiple_of(blk * T, T), T)
        ready = sends(r, c0, start)
        pl.when(turn == 0)(lambda: locals_[2].wait())
        kv[0, keys_at, :] = jnp.dot(nm[...], wkv[...], preferred_element_type=F32).astype(BF16)
        ready(0)
        pl.when(turn == 0)(lambda: locals_[3].wait())
        kv[1, keys_at, :] = jnp.dot(nm[...], wvv[...], preferred_element_type=F32).astype(BF16)
        ready(1)

        @pl.when(turn == 0)
        def _():
            locals_[4].wait()
            qs[...] = jnp.dot(nm[...], wqv[...], preferred_element_type=F32).astype(BF16)
            agg_ref[...] = lt[:, pl.ds(pl.multiple_of(s * share, share), share)].astype(BF16)

        return carry

    lax.fori_loop(0, C, own_block, 0)
    ms[...] = jnp.full(ms.shape, -1e30, F32)
    ls[...] = jnp.zeros(ls.shape, F32)
    acc[...] = jnp.zeros(acc.shape, F32)
    scale = 1.0 / math.sqrt(HEAD_DIM)

    def attend(row):
        keys_at = pl.ds(pl.multiple_of(row * W, W), W)
        for h in range(H):
            cols = slice(h * HEAD_DIM, (h + 1) * HEAD_DIM)
            logits = (
                lax.dot_general(
                    qs[:, cols], kv[0, keys_at, cols], (((1,), (1,)), ((), ())),
                    preferred_element_type=F32,
                )
                * scale
            )
            old = ms[h]
            fresh = jnp.maximum(old, jnp.max(logits, axis=1, keepdims=True))
            shrink = jnp.exp(old - fresh)
            expo = jnp.exp(logits - fresh[:, 0:1])
            ls[h] = ls[h] * shrink + jnp.sum(expo, axis=1, keepdims=True)
            ms[h] = fresh
            acc[:, cols] = acc[:, cols] * shrink[:, 0:1] + jnp.dot(
                expo.astype(BF16), kv[1, keys_at, cols], preferred_element_type=F32
            )

    def from_column(row):
        for part in range(2):
            arrived(part, (row * C + col) * 2 + c)
            sends(row, col, start)(part)

    def finish(row):
        for dist in range(1, C):
            for way in (-1, 1):
                c0 = col + way * dist

                @pl.when((row != r) & (c0 >= 0) & (c0 < C))
                def _():
                    for part in range(2):
                        arrived(part, (row * C + c0) * 2 + c)
                        sends(row, c0, start)(part)

        for c0 in range(C):
            for part in range(2):
                arrived(part, (row * C + c0) * 2 + 1 - c)
        attend(row)

    def stage(d, carry):
        def ahead(way, inner):
            row = r + (2 * way - 1) * (d + 1)
            pl.when((row >= 0) & (row < R))(lambda: from_column(row))
            return inner

        lax.fori_loop(0, 2, ahead, 0)

        def now(way, inner):
            row = r + (2 * way - 1) * d
            pl.when((row >= 0) & (row < R) & (d + way > 0))(lambda: finish(row))
            return inner

        lax.fori_loop(0, 2, now, 0)
        return carry

    lax.fori_loop(0, R, stage, 0)

    for h in range(H):
        cols = slice(h * HEAD_DIM, (h + 1) * HEAD_DIM)
        ho[s, :, cols] = (acc[:, cols] / ls[h][:, 0:1]).astype(BF16)
    h_out = [remote(ho.at[s], ho.at[s], h_s.at[k], h_r.at[k], seg_at(k), b) for k in range(1, S)]
    for one in h_out:
        one.start()
    op_out = []
    for k in range(1, S):
        src = seg_at(S - k)
        block = woa.at[src, wo_rows(c)]
        remote(block, block, o_s.at[k], o_r.at[k], s, partner).wait_recv()
        one = remote(block, block, op_s.at[k], op_r.at[k], s, partner)
        one.start()
        op_out.append(one)
    locals_[5].wait()
    lt[:, 0:share] = jnp.dot(ho[s], woa[s], preferred_element_type=F32)
    for k in range(1, S):
        src = seg_at(S - k)
        block = woa.at[src, wo_rows(1 - c)]
        remote(block, block, op_s.at[k], op_r.at[k], s, partner).wait_recv()
        remote(ho.at[src], ho.at[src], h_s.at[k], h_r.at[k], s, partner).wait_recv()
        lt[:, 0:share] = lt[:, 0:share] + jnp.dot(ho[src], woa[src], preferred_element_type=F32)
    att_ref[...] = lt[:, 0:share].astype(BF16)

    for one in e_out + ep_out + c_out + y_out + o_out + op_out + h_out:
        one.wait_send()

    def drain(i, carry):
        ends = sends(i // C, lax.rem(i, C), lambda copy: copy.wait_send())
        ends(0)
        ends(1)
        return carry

    lax.fori_loop(0, R * C, drain, 0)


def solution(mesh):
    S = mesh.shape["segment"]
    B = mesh.shape["blk"]
    chips = B // 2
    C = 1
    while C * C * 4 <= chips:
        C *= 2
    R = chips // C

    def on_device(
        pixels, var_group, var_embed, group_weight, agg_query, lat_index, lat_table, norm_gain,
        w_query, w_key, w_value, w_out,
    ):
        vl, D = var_embed.shape
        G, PX, _ = group_weight.shape
        T = pixels.shape[2]
        NL = lat_table.shape[0]
        cl = w_query.shape[1]
        H = cl // HEAD_DIM
        share = D // S
        kp = ((S * vl + G * PX + 8 + 127) // 128) * 128
        vm = pl.BlockSpec(memory_space=pltpu.VMEM)
        far = pl.BlockSpec(memory_space=pltpu.HBM)
        dma = pltpu.SemaphoreType.DMA
        out = jax.ShapeDtypeStruct((T, share), BF16)
        return pl.pallas_call(
            functools.partial(kernel, S, R, C),
            out_shape=(out, out),
            in_specs=[far] * 12,
            out_specs=(vm, vm),
            scratch_shapes=[
                pltpu.VMEM((vl, PX, T), BF16),
                pltpu.VMEM((1, vl), jnp.int32),
                pltpu.VMEM((G, PX, D), BF16),
                pltpu.VMEM((1, D), F32),
                pltpu.VMEM((1, T), jnp.int32),
                pltpu.VMEM((1, D), F32),
                pltpu.VMEM((kp, D), BF16),
                pltpu.VMEM((NL, D), BF16),
                pltpu.VMEM((D, cl), BF16),
                pltpu.VMEM((D, cl), BF16),
                pltpu.VMEM((D, cl), BF16),
                pltpu.VMEM((S, cl, share), BF16),
                pltpu.VMEM((G * PX, D), F32),
                pltpu.VMEM((vl * PX, T), F32),
                pltpu.VMEM((S, vl + G * PX + 16, T), F32),
                pltpu.VMEM((C, kp, T), F32),
                pltpu.VMEM((T, D), F32),
                pltpu.VMEM((T, D), BF16),
                pltpu.VMEM((2, B * T, cl), BF16),
                pltpu.VMEM((T, cl), BF16),
                pltpu.VMEM((H, T, 128), F32),
                pltpu.VMEM((H, T, 128), F32),
                pltpu.VMEM((T, cl), F32),
                pltpu.VMEM((S, T, cl), BF16),
                dma((12,)),
            ]
            + [dma((S,))] * 12
            + [dma((C,)), dma((C,)), dma((5, 2, B)), dma((2, B))],
            compiler_params=pltpu.CompilerParams(
                collective_id=0, has_side_effects=True, vmem_limit_bytes=48 * 1024 * 1024
            ),
        )(
            pixels,
            var_group.reshape(1, vl),
            var_embed,
            group_weight,
            agg_query.astype(F32).reshape(1, D),
            lat_index.reshape(1, T),
            lat_table,
            norm_gain.reshape(1, D),
            w_query,
            w_key,
            w_value,
            w_out,
        )

    in_specs = (
        P("segment", None, "blk"), P("segment"), P("segment", None), P(), P(), P("blk"), P(), P(),
        P(None, "segment"), P(None, "segment"), P(None, "segment"), P("segment", None),
    )
    out_specs = (P("blk", "segment"), P("blk", "segment"))
    return jax.shard_map(
        on_device, mesh=mesh, in_specs=in_specs, out_specs=out_specs, check_vma=False
    )
```

```python
import functools
import math

import jax
import jax.numpy as jnp
from jax import lax
from jax.experimental import pallas as pl
from jax.experimental.pallas import tpu as pltpu
from jax.sharding import PartitionSpec as P

HEAD_DIM = 128
MESH = pl.DeviceIdType.MESH
F32 = jnp.float32
BF16 = jnp.bfloat16


def kernel(
    S, R, C,
    pix_hbm, vg_hbm, emb_ref, gw_hbm, q_hbm, lidx_hbm, lat_ref, gain_hbm,
    wq_ref, wk_ref, wv_ref, wo_ref,
    agg_ref, att_ref,
    pix_ref, vg_ref, gw_ref, q_ref, lidx_ref, gain_ref,
    bm, latv, wqv, wkv, wvv, woa, gtmp, pixf, cf, ck, lt, nm, kv, qs, ms, ls, acc, ho,
    loc, e_s, e_r, ep_s, ep_r, c_s, c_r, o_s, o_r, op_s, op_r, h_s, h_r, y_s, y_r, k_s, k_r,
):
    D = emb_ref.shape[1]
    Vl = emb_ref.shape[0]
    G, PX, _ = gw_ref.shape
    GP = G * PX
    T = pix_ref.shape[2]
    NL = lat_ref.shape[0]
    Cl = wq_ref.shape[1]
    H = Cl // HEAD_DIM
    share = D // S
    half = D // 2
    clh = Cl // 2
    Kp = ck.shape[1]
    used = S * Vl + GP
    W = C * 2 * T
    s = lax.axis_index("segment")
    b = lax.axis_index("blk")
    c = lax.rem(b, 2)
    rc = b // 2
    col = lax.rem(rc, C)
    r = rc // C
    partner = b + 1 - 2 * c

    def dev(seg, blk):
        return {"segment": seg, "blk": blk}

    barrier = pltpu.get_barrier_semaphore()

    def greet(seg, blk):
        pl.semaphore_signal(barrier, inc=1, device_id=dev(seg, blk), device_id_type=MESH)

    for k in range(1, S):
        greet(lax.rem(s + k, S), b)
    greet(s, partner)
    chips = R * C

    def greet_chip(k, carry):
        greet(s, lax.rem(rc + k, chips) * 2 + c)
        return carry

    lax.fori_loop(1, chips, greet_chip, 0)

    own_rows = pl.ds(pl.multiple_of(s * Vl, Vl), Vl)
    small = [
        pltpu.make_async_copy(src, dst, loc.at[6 + i])
        for i, (src, dst) in enumerate(
            [(gw_hbm, gw_ref), (q_hbm, q_ref), (pix_hbm, pix_ref), (vg_hbm, vg_ref),
             (lidx_hbm, lidx_ref), (gain_hbm, gain_ref)]
        )
    ]
    for one in small[:2]:
        one.start()
    locals_ = [
        pltpu.make_async_copy(emb_ref, bm.at[own_rows], loc.at[0]),
        pltpu.make_async_copy(lat_ref, latv, loc.at[1]),
        pltpu.make_async_copy(wk_ref, wkv, loc.at[2]),
        pltpu.make_async_copy(wv_ref, wvv, loc.at[3]),
        pltpu.make_async_copy(wq_ref, wqv, loc.at[4]),
        pltpu.make_async_copy(
            wo_ref.at[:, pl.ds(pl.multiple_of(s * share, share), share)], woa.at[s], loc.at[5]
        ),
    ]
    locals_[0].start()
    for one in small[2:] + locals_[1:]:
        one.start()
    count = S + chips - 1
    pl.semaphore_wait(barrier, count)

    def remote(src, dst, send, recv, seg, blk):
        return pltpu.make_async_remote_copy(
            src_ref=src, dst_ref=dst, send_sem=send, recv_sem=recv,
            device_id=dev(seg, blk), device_id_type=MESH,
        )

    def seg_at(k):
        return lax.rem(s + k, S)

    def emb_region(seg, core):
        return bm.at[
            pl.ds(pl.multiple_of(seg * Vl, Vl), Vl), pl.ds(pl.multiple_of(core * half, half), half)
        ]

    my_half = pl.ds(pl.multiple_of(c * half, half), half)
    e_out = [
        remote(emb_ref.at[:, my_half], emb_region(s, c), e_s.at[k], e_r.at[k], seg_at(k), b)
        for k in range(1, S)
    ]
    for one in e_out:
        one.start()

    small[1].wait()
    q = q_ref[...]
    small[0].wait()
    for g in range(G):
        one_group = gw_ref[g].astype(F32)
        for p in range(PX):
            gtmp[p * G + g : p * G + g + 1, :] = one_group[p : p + 1, :]
    gwp = gtmp[...]
    bm[S * Vl : S * Vl + GP, :] = gwp.astype(BF16)
    if Kp > S * Vl + GP:
        bm[S * Vl + GP : Kp, :] = jnp.zeros((Kp - S * Vl - GP, D), BF16)
    pg = jnp.sum(gwp * q, axis=1, keepdims=True)
    small[2].wait()
    for v in range(Vl):
        pixf[PX * v : PX * v + PX, :] = pix_ref[v].astype(F32)
    small[3].wait()
    vg = vg_ref[...]
    row_at = lax.broadcasted_iota(jnp.int32, (Vl, Vl), 0)
    col_at = lax.broadcasted_iota(jnp.int32, (Vl, Vl), 1)
    vcol = jnp.sum(jnp.where(row_at == col_at, vg.astype(F32), 0.0), axis=1, keepdims=True)
    onehot = (lax.broadcasted_iota(jnp.int32, (G, Vl), 0) == vg).astype(F32)
    locals_[0].wait()
    scores = jnp.sum(bm[own_rows, :].astype(F32) * q, axis=1, keepdims=True)
    planes = [pixf[pl.ds(p, Vl, stride=PX), :] for p in range(PX)]
    for p in range(PX):
        pv = jnp.zeros((Vl, 1), F32)
        for g in range(G):
            pv = jnp.where(vcol == float(g), pg[p * G + g : p * G + g + 1, :], pv)
        scores = scores + planes[p] * pv
    scores = scores / math.sqrt(D)
    peak = jnp.max(scores, axis=0, keepdims=True)
    expo = jnp.exp(scores - peak)
    cf[s, 0:Vl, :] = expo
    for p in range(PX):
        cf[s, Vl + p * G : Vl + p * G + G, :] = jnp.dot(
            onehot, expo * planes[p], precision=lax.Precision.HIGHEST, preferred_element_type=F32
        )
    top = Vl + GP
    cf[s, top : top + 8, :] = jnp.broadcast_to(peak, (8, T))
    cf[s, top + 8 : top + 16, :] = jnp.broadcast_to(jnp.sum(expo, axis=0, keepdims=True), (8, T))
    c_out = [
        remote(cf.at[s], cf.at[s], c_s.at[k], c_r.at[k], seg_at(k), b) for k in range(1, S)
    ]
    for one in c_out:
        one.start()

    def wo_rows(core):
        return pl.ds(pl.multiple_of(core * clh, clh), clh)

    o_out = [
        remote(
            wo_ref.at[wo_rows(c), pl.ds(pl.multiple_of(seg_at(k) * share, share), share)],
            woa.at[s, wo_rows(c)], o_s.at[k], o_r.at[k], seg_at(k), b,
        )
        for k in range(1, S)
    ]
    for one in o_out:
        one.start()

    small[4].wait()
    ck[rc, used : used + 8, :] = jnp.broadcast_to(lidx_ref[...].astype(F32), (8, T))
    if Kp > used + 8:

        def clear(i, carry):
            ck[i, used + 8 : Kp, :] = jnp.zeros((Kp - used - 8, T), F32)
            return carry

        lax.fori_loop(0, chips, clear, 0)

    ep_out = []
    for k in range(1, S):
        src = seg_at(S - k)
        remote(emb_region(src, c), emb_region(src, c), e_s.at[k], e_r.at[k], s, partner).wait_recv()
        one = remote(
            emb_region(src, c), emb_region(src, c), ep_s.at[k], ep_r.at[k], s, partner
        )
        one.start()
        ep_out.append(one)
    for k in range(1, S):
        src = seg_at(S - k)
        remote(cf.at[src], cf.at[src], c_s.at[k], c_r.at[k], s, partner).wait_recv()
    best = cf[0, top : top + 1, :]
    for k in range(1, S):
        best = jnp.maximum(best, cf[k, top : top + 1, :])
    factors = [jnp.exp(cf[k, top : top + 1, :] - best) for k in range(S)]
    total = factors[0] * cf[0, top + 8 : top + 9, :]
    for k in range(1, S):
        total = total + factors[k] * cf[k, top + 8 : top + 9, :]
    grouped = jnp.zeros((GP, T), F32)
    for k in range(S):
        share_k = factors[k] / total
        ck[rc, k * Vl : k * Vl + Vl, :] = cf[k, 0:Vl, :] * share_k
        grouped = grouped + cf[k, Vl : Vl + GP, :] * share_k
    ck[rc, S * Vl : used, :] = grouped
    mine = ck.at[rc, pl.ds(0, used + 8)]

    def spread_to(dist, row_way, act):
        row = r + (2 * row_way - 1) * dist

        @pl.when((row >= 0) & (row < R) & (dist + row_way > 0))
        def _():
            def one_col(k, carry):
                chip = row * C + lax.rem(col + k, C)

                @pl.when(chip != rc)
                def _():
                    act(remote(mine, mine, y_s.at[chip], y_r.at[rc], s, chip * 2 + c))

                return carry

            lax.fori_loop(0, C, one_col, 0)

    def all_chips(act):
        def outer(i, carry):
            spread_to(i // 2, lax.rem(i, 2), act)
            return carry

        lax.fori_loop(0, 2 * R, outer, 0)

    all_chips(lambda copy: copy.start())
    small[5].wait()

    def region(part, blk):
        return kv.at[part, pl.ds(pl.multiple_of(blk * T, T), T)]

    def shared(part, blk):
        return remote(
            region(part, blk), region(part, blk), k_s.at[part, blk], k_r.at[part, blk],
            s, partner,
        )

    lat_rows = ((NL + 127) // 128) * 128
    step = 256

    def pieces(x):
        hi = x.astype(BF16)
        rest = x - hi.astype(F32)
        mid = rest.astype(BF16)
        return hi, mid, (rest - mid.astype(F32)).astype(BF16)

    def compute(row, first):
        split = []
        for c0 in range(C):
            chip = row * C + c0

            @pl.when(chip != rc)
            def _():
                there = ck.at[chip, pl.ds(0, used + 8)]
                remote(there, there, y_s.at[chip], y_r.at[chip], s, partner).wait_recv()

            at_row = ck[chip, used : used + 1, :]
            rows = lax.broadcasted_iota(jnp.int32, (lat_rows, T), 0).astype(F32)
            hot = (rows == at_row).astype(F32).T.astype(BF16)[:, :NL]
            split.append(pieces(ck[chip].T) + (hot,))
        hi, mid, low, hot = [jnp.concatenate(x, axis=0) for x in zip(*split)]

        @pl.when(first)
        def _():
            for k in range(1, S):
                other = emb_region(seg_at(S - k), 1 - c)
                remote(other, other, ep_s.at[k], ep_r.at[k], s, partner).wait_recv()
            locals_[1].wait()

        mean = jnp.zeros((C * T, 1), F32)
        for j in range(D // step):
            at = slice(j * step, (j + 1) * step)
            base = bm[:, at]
            part = jnp.dot(low, base, preferred_element_type=F32)
            part = part + jnp.dot(mid, base, preferred_element_type=F32)
            part = part + jnp.dot(hi, base, preferred_element_type=F32)
            part = part + jnp.dot(hot, latv[:, at], preferred_element_type=F32)
            lt[:, at] = part
            mean = mean + jnp.sum(part, axis=1, keepdims=True)
        mean = mean / D
        spread = jnp.zeros((C * T, 1), F32)
        for j in range(D // step):
            center = lt[:, j * step : (j + 1) * step] - mean
            spread = spread + jnp.sum(center * center, axis=1, keepdims=True)
        inv = lax.rsqrt(spread / D + 1e-05)
        for j in range(D // step):
            at = slice(j * step, (j + 1) * step)
            nm[:, at] = ((lt[:, at] - mean) * inv * gain_ref[:, at]).astype(BF16)
        for part, weight in ((0, wkv), (1, wvv)):
            pl.when(first)(lambda: locals_[2 + part].wait())
            made = jnp.dot(nm[...], weight[...], preferred_element_type=F32).astype(BF16)
            for c0 in range(C):
                blk = (row * C + c0) * 2 + c
                kv[part, pl.ds(pl.multiple_of(blk * T, T), T), :] = made[c0 * T : (c0 + 1) * T]
                shared(part, blk).start()

        @pl.when(first)
        def _():
            locals_[4].wait()
            own = pl.ds(pl.multiple_of(col * T, T), T)
            qs[...] = jnp.dot(nm[own, :], wqv[...], preferred_element_type=F32).astype(BF16)
            agg_ref[...] = lt[own, pl.ds(pl.multiple_of(s * share, share), share)].astype(BF16)

    ms[...] = jnp.full(ms.shape, -1e30, F32)
    ls[...] = jnp.zeros(ls.shape, F32)
    acc[...] = jnp.zeros(acc.shape, F32)
    scale = 1.0 / math.sqrt(HEAD_DIM)

    def attend(row):
        keys_at = pl.ds(pl.multiple_of(row * W, W), W)
        for h in range(H):
            cols = slice(h * HEAD_DIM, (h + 1) * HEAD_DIM)
            logits = (
                lax.dot_general(
                    qs[:, cols], kv[0, keys_at, cols], (((1,), (1,)), ((), ())),
                    preferred_element_type=F32,
                )
                * scale
            )
            old = ms[h]
            fresh = jnp.maximum(old, jnp.max(logits, axis=1, keepdims=True))
            shrink = jnp.exp(old - fresh)
            expo = jnp.exp(logits - fresh[:, 0:1])
            ls[h] = ls[h] * shrink + jnp.sum(expo, axis=1, keepdims=True)
            ms[h] = fresh
            acc[:, cols] = acc[:, cols] * shrink[:, 0:1] + jnp.dot(
                expo.astype(BF16), kv[1, keys_at, cols], preferred_element_type=F32
            )

    def finish(row):
        for c0 in range(C):
            for part in range(2):
                shared(part, (row * C + c0) * 2 + 1 - c).wait_recv()
        attend(row)

    def turn(i, before):
        dist, way = (i + 1) // 2, lax.rem(i, 2)
        row = r + (1 - 2 * way) * dist
        real = (row >= 0) & (row < R)

        @pl.when(real)
        def _():
            compute(row, i == 0)
            pl.when(i > 0)(lambda: finish(before))

        return jnp.where(real, row, before)

    finish(lax.fori_loop(0, 2 * R - 1, turn, r))

    for h in range(H):
        cols = slice(h * HEAD_DIM, (h + 1) * HEAD_DIM)
        ho[s, :, cols] = (acc[:, cols] / ls[h][:, 0:1]).astype(BF16)
    h_out = [remote(ho.at[s], ho.at[s], h_s.at[k], h_r.at[k], seg_at(k), b) for k in range(1, S)]
    for one in h_out:
        one.start()
    op_out = []
    for k in range(1, S):
        src = seg_at(S - k)
        block = woa.at[src, wo_rows(c)]
        remote(block, block, o_s.at[k], o_r.at[k], s, partner).wait_recv()
        one = remote(block, block, op_s.at[k], op_r.at[k], s, partner)
        one.start()
        op_out.append(one)
    locals_[5].wait()
    lt[0:T, 0:share] = jnp.dot(ho[s], woa[s], preferred_element_type=F32)
    for k in range(1, S):
        src = seg_at(S - k)
        block = woa.at[src, wo_rows(1 - c)]
        remote(block, block, op_s.at[k], op_r.at[k], s, partner).wait_recv()
        remote(ho.at[src], ho.at[src], h_s.at[k], h_r.at[k], s, partner).wait_recv()
        lt[0:T, 0:share] = lt[0:T, 0:share] + jnp.dot(ho[src], woa[src], preferred_element_type=F32)
    att_ref[...] = lt[0:T, 0:share].astype(BF16)

    for one in e_out + ep_out + c_out + o_out + op_out + h_out:
        one.wait_send()

    all_chips(lambda copy: copy.wait_send())

    def drain(i, carry):
        shared(0, i * 2 + c).wait_send()
        shared(1, i * 2 + c).wait_send()
        return carry

    lax.fori_loop(0, chips, drain, 0)


def solution(mesh):
    S = mesh.shape["segment"]
    B = mesh.shape["blk"]
    chips = B // 2
    C = 1
    while C * C * 4 <= chips:
        C *= 2
    R = chips // C

    def on_device(
        pixels, var_group, var_embed, group_weight, agg_query, lat_index, lat_table, norm_gain,
        w_query, w_key, w_value, w_out,
    ):
        vl, D = var_embed.shape
        G, PX, _ = group_weight.shape
        T = pixels.shape[2]
        NL = lat_table.shape[0]
        cl = w_query.shape[1]
        H = cl // HEAD_DIM
        share = D // S
        kp = ((S * vl + G * PX + 8 + 127) // 128) * 128
        vm = pl.BlockSpec(memory_space=pltpu.VMEM)
        far = pl.BlockSpec(memory_space=pltpu.HBM)
        dma = pltpu.SemaphoreType.DMA
        out = jax.ShapeDtypeStruct((T, share), BF16)
        return pl.pallas_call(
            functools.partial(kernel, S, R, C),
            out_shape=(out, out),
            in_specs=[far] * 12,
            out_specs=(vm, vm),
            scratch_shapes=[
                pltpu.VMEM((vl, PX, T), BF16),
                pltpu.VMEM((1, vl), jnp.int32),
                pltpu.VMEM((G, PX, D), BF16),
                pltpu.VMEM((1, D), F32),
                pltpu.VMEM((1, T), jnp.int32),
                pltpu.VMEM((1, D), F32),
                pltpu.VMEM((kp, D), BF16),
                pltpu.VMEM((NL, D), BF16),
                pltpu.VMEM((D, cl), BF16),
                pltpu.VMEM((D, cl), BF16),
                pltpu.VMEM((D, cl), BF16),
                pltpu.VMEM((S, cl, share), BF16),
                pltpu.VMEM((G * PX, D), F32),
                pltpu.VMEM((vl * PX, T), F32),
                pltpu.VMEM((S, vl + G * PX + 16, T), F32),
                pltpu.VMEM((chips, kp, T), F32),
                pltpu.VMEM((C * T, D), F32),
                pltpu.VMEM((C * T, D), BF16),
                pltpu.VMEM((2, B * T, cl), BF16),
                pltpu.VMEM((T, cl), BF16),
                pltpu.VMEM((H, T, 128), F32),
                pltpu.VMEM((H, T, 128), F32),
                pltpu.VMEM((T, cl), F32),
                pltpu.VMEM((S, T, cl), BF16),
                dma((12,)),
            ]
            + [dma((S,))] * 12
            + [dma((chips,)), dma((chips,)), dma((2, B)), dma((2, B))],
            compiler_params=pltpu.CompilerParams(
                collective_id=0, has_side_effects=True, vmem_limit_bytes=67_043_328
            ),
        )(
            pixels,
            var_group.reshape(1, vl),
            var_embed,
            group_weight,
            agg_query.astype(F32).reshape(1, D),
            lat_index.reshape(1, T),
            lat_table,
            norm_gain.reshape(1, D),
            w_query,
            w_key,
            w_value,
            w_out,
        )

    in_specs = (
        P("segment", None, "blk"), P("segment"), P("segment", None), P(), P(), P("blk"), P(), P(),
        P(None, "segment"), P(None, "segment"), P(None, "segment"), P("segment", None),
    )
    out_specs = (P("blk", "segment"), P("blk", "segment"))
    return jax.shard_map(
        on_device, mesh=mesh, in_specs=in_specs, out_specs=out_specs, check_vma=False
    )
```

```python
import functools
import math

import jax
import jax.numpy as jnp
from jax import lax
from jax.experimental import pallas as pl
from jax.experimental.pallas import tpu as pltpu
from jax.sharding import PartitionSpec as P

HEAD_DIM = 128
MESH = pl.DeviceIdType.MESH
F32 = jnp.float32
BF16 = jnp.bfloat16


def kernel(
    S, R, C,
    pix_hbm, vg_hbm, emb_ref, gw_hbm, q_hbm, lidx_hbm, lat_ref, gain_hbm,
    wq_ref, wk_ref, wv_ref, wo_ref,
    agg_ref, att_ref,
    pix_ref, vg_ref, gw_ref, q_ref, lidx_ref, gain_ref,
    bm, latv, wqv, wkv, wvv, woa, gtmp, pixf, cf, ck, lt, nm, kv, qs, ms, ls, acc, ho,
    loc, e_s, e_r, ep_s, ep_r, c_s, c_r, o_s, o_r, op_s, op_r, h_s, h_r, y_s, y_r, k_s, k_r,
):
    D = emb_ref.shape[1]
    Vl = emb_ref.shape[0]
    G, PX, _ = gw_ref.shape
    GP = G * PX
    T = pix_ref.shape[2]
    NL = lat_ref.shape[0]
    Cl = wq_ref.shape[1]
    H = Cl // HEAD_DIM
    share = D // S
    half = D // 2
    clh = Cl // 2
    Kp = ck.shape[1]
    used = S * Vl + GP
    W = C * 2 * T
    s = lax.axis_index("segment")
    b = lax.axis_index("blk")
    c = lax.rem(b, 2)
    rc = b // 2
    col = lax.rem(rc, C)
    r = rc // C
    partner = b + 1 - 2 * c

    def dev(seg, blk):
        return {"segment": seg, "blk": blk}

    barrier = pltpu.get_barrier_semaphore()

    def greet(seg, blk):
        pl.semaphore_signal(barrier, inc=1, device_id=dev(seg, blk), device_id_type=MESH)

    for k in range(1, S):
        greet(lax.rem(s + k, S), b)
    greet(s, partner)
    chips = R * C

    def greet_chip(k, carry):
        greet(s, lax.rem(rc + k, chips) * 2 + c)
        return carry

    lax.fori_loop(1, chips, greet_chip, 0)

    own_rows = pl.ds(pl.multiple_of(s * Vl, Vl), Vl)
    small = [
        pltpu.make_async_copy(src, dst, loc.at[6 + i])
        for i, (src, dst) in enumerate(
            [(gw_hbm, gw_ref), (q_hbm, q_ref), (pix_hbm, pix_ref), (vg_hbm, vg_ref),
             (lidx_hbm, lidx_ref), (gain_hbm, gain_ref)]
        )
    ]
    for one in small[:2]:
        one.start()
    locals_ = [
        pltpu.make_async_copy(emb_ref, bm.at[own_rows], loc.at[0]),
        pltpu.make_async_copy(lat_ref, latv, loc.at[1]),
        pltpu.make_async_copy(wk_ref, wkv, loc.at[2]),
        pltpu.make_async_copy(wv_ref, wvv, loc.at[3]),
        pltpu.make_async_copy(wq_ref, wqv, loc.at[4]),
        pltpu.make_async_copy(
            wo_ref.at[:, pl.ds(pl.multiple_of(s * share, share), share)], woa.at[s], loc.at[5]
        ),
    ]
    locals_[0].start()
    for one in small[2:] + locals_[1:]:
        one.start()
    count = S + chips - 1
    pl.semaphore_wait(barrier, count)

    def remote(src, dst, send, recv, seg, blk):
        return pltpu.make_async_remote_copy(
            src_ref=src, dst_ref=dst, send_sem=send, recv_sem=recv,
            device_id=dev(seg, blk), device_id_type=MESH,
        )

    def seg_at(k):
        return lax.rem(s + k, S)

    def emb_region(seg, core):
        return bm.at[
            pl.ds(pl.multiple_of(seg * Vl, Vl), Vl), pl.ds(pl.multiple_of(core * half, half), half)
        ]

    my_half = pl.ds(pl.multiple_of(c * half, half), half)
    e_out = [
        remote(emb_ref.at[:, my_half], emb_region(s, c), e_s.at[k], e_r.at[k], seg_at(k), b)
        for k in range(1, S)
    ]
    for one in e_out:
        one.start()

    small[1].wait()
    q = q_ref[...]
    small[0].wait()
    for g in range(G):
        one_group = gw_ref[g].astype(F32)
        for p in range(PX):
            gtmp[p * G + g : p * G + g + 1, :] = one_group[p : p + 1, :]
    gwp = gtmp[...]
    bm[S * Vl : S * Vl + GP, :] = gwp.astype(BF16)
    if Kp > S * Vl + GP:
        bm[S * Vl + GP : Kp, :] = jnp.zeros((Kp - S * Vl - GP, D), BF16)
    pg = jnp.sum(gwp * q, axis=1, keepdims=True)
    small[2].wait()
    for v in range(Vl):
        pixf[PX * v : PX * v + PX, :] = pix_ref[v].astype(F32)
    small[3].wait()
    vg = vg_ref[...]
    row_at = lax.broadcasted_iota(jnp.int32, (Vl, Vl), 0)
    col_at = lax.broadcasted_iota(jnp.int32, (Vl, Vl), 1)
    vcol = jnp.sum(jnp.where(row_at == col_at, vg.astype(F32), 0.0), axis=1, keepdims=True)
    onehot = (lax.broadcasted_iota(jnp.int32, (G, Vl), 0) == vg).astype(F32)
    locals_[0].wait()
    scores = jnp.sum(bm[own_rows, :].astype(F32) * q, axis=1, keepdims=True)
    planes = [pixf[pl.ds(p, Vl, stride=PX), :] for p in range(PX)]
    for p in range(PX):
        pv = jnp.zeros((Vl, 1), F32)
        for g in range(G):
            pv = jnp.where(vcol == float(g), pg[p * G + g : p * G + g + 1, :], pv)
        scores = scores + planes[p] * pv
    scores = scores / math.sqrt(D)
    peak = jnp.max(scores, axis=0, keepdims=True)
    expo = jnp.exp(scores - peak)
    cf[s, 0:Vl, :] = expo
    for p in range(PX):
        cf[s, Vl + p * G : Vl + p * G + G, :] = jnp.dot(
            onehot, expo * planes[p], precision=lax.Precision.HIGHEST, preferred_element_type=F32
        )
    top = Vl + GP
    cf[s, top : top + 8, :] = jnp.broadcast_to(peak, (8, T))
    cf[s, top + 8 : top + 16, :] = jnp.broadcast_to(jnp.sum(expo, axis=0, keepdims=True), (8, T))
    c_out = [
        remote(cf.at[s], cf.at[s], c_s.at[k], c_r.at[k], seg_at(k), b) for k in range(1, S)
    ]
    for one in c_out:
        one.start()

    def wo_rows(core):
        return pl.ds(pl.multiple_of(core * clh, clh), clh)

    o_out = [
        remote(
            wo_ref.at[wo_rows(c), pl.ds(pl.multiple_of(seg_at(k) * share, share), share)],
            woa.at[s, wo_rows(c)], o_s.at[k], o_r.at[k], seg_at(k), b,
        )
        for k in range(1, S)
    ]
    for one in o_out:
        one.start()

    small[4].wait()
    ck[rc, used : used + 8, :] = jnp.broadcast_to(lidx_ref[...].astype(F32), (8, T))
    if Kp > used + 8:

        def clear(i, carry):
            ck[i, used + 8 : Kp, :] = jnp.zeros((Kp - used - 8, T), F32)
            return carry

        lax.fori_loop(0, chips, clear, 0)

    ep_out = []
    for k in range(1, S):
        src = seg_at(S - k)
        remote(emb_region(src, c), emb_region(src, c), e_s.at[k], e_r.at[k], s, partner).wait_recv()
        one = remote(
            emb_region(src, c), emb_region(src, c), ep_s.at[k], ep_r.at[k], s, partner
        )
        one.start()
        ep_out.append(one)
    for k in range(1, S):
        src = seg_at(S - k)
        remote(cf.at[src], cf.at[src], c_s.at[k], c_r.at[k], s, partner).wait_recv()
    best = cf[0, top : top + 1, :]
    for k in range(1, S):
        best = jnp.maximum(best, cf[k, top : top + 1, :])
    factors = [jnp.exp(cf[k, top : top + 1, :] - best) for k in range(S)]
    total = factors[0] * cf[0, top + 8 : top + 9, :]
    for k in range(1, S):
        total = total + factors[k] * cf[k, top + 8 : top + 9, :]
    grouped = jnp.zeros((GP, T), F32)
    for k in range(S):
        share_k = factors[k] / total
        ck[rc, k * Vl : k * Vl + Vl, :] = cf[k, 0:Vl, :] * share_k
        grouped = grouped + cf[k, Vl : Vl + GP, :] * share_k
    ck[rc, S * Vl : used, :] = grouped
    mine = ck.at[rc, pl.ds(0, used + 8)]

    def spread_to(dist, row_way, act):
        row = r + (2 * row_way - 1) * dist

        @pl.when((row >= 0) & (row < R) & (dist + row_way > 0))
        def _():
            def one_col(k, carry):
                chip = row * C + lax.rem(col + k, C)

                @pl.when(chip != rc)
                def _():
                    act(remote(mine, mine, y_s.at[chip], y_r.at[rc], s, chip * 2 + c))

                return carry

            lax.fori_loop(0, C, one_col, 0)

    def all_chips(act):
        def outer(i, carry):
            spread_to(i // 2, lax.rem(i, 2), act)
            return carry

        lax.fori_loop(0, 2 * R, outer, 0)

    all_chips(lambda copy: copy.start())
    small[5].wait()

    def region(part, blk):
        return kv.at[part, pl.ds(pl.multiple_of(blk * T, T), T)]

    def shared(part, blk):
        return remote(
            region(part, blk), region(part, blk), k_s.at[part, blk], k_r.at[part, blk],
            s, partner,
        )

    lat_rows = ((NL + 127) // 128) * 128
    step = 512

    def pieces(x):
        hi = x.astype(BF16)
        rest = x - hi.astype(F32)
        mid = rest.astype(BF16)
        return hi, mid, (rest - mid.astype(F32)).astype(BF16)

    def compute(row, first):
        split = []
        for c0 in range(C):
            chip = row * C + c0

            @pl.when(chip != rc)
            def _():
                there = ck.at[chip, pl.ds(0, used + 8)]
                remote(there, there, y_s.at[chip], y_r.at[chip], s, partner).wait_recv()

            at_row = ck[chip, used : used + 1, :]
            rows = lax.broadcasted_iota(jnp.int32, (lat_rows, T), 0).astype(F32)
            hot = (rows == at_row).astype(F32).T.astype(BF16)[:, :NL]
            split.append(pieces(ck[chip].T) + (hot,))
        hi, mid, low, hot = [jnp.concatenate(x, axis=0) for x in zip(*split)]
        stacked = jnp.concatenate([low, mid, hi], axis=0)
        rows_c = C * T

        @pl.when(first)
        def _():
            for k in range(1, S):
                other = emb_region(seg_at(S - k), 1 - c)
                remote(other, other, ep_s.at[k], ep_r.at[k], s, partner).wait_recv()
            locals_[1].wait()

        mean = jnp.zeros((C * T, 1), F32)
        for j in range(D // step):
            at = slice(j * step, (j + 1) * step)
            base = bm[:, at]
            three = jnp.dot(stacked, base, preferred_element_type=F32)
            part = three[0:rows_c] + three[rows_c : 2 * rows_c] + three[2 * rows_c :]
            part = part + jnp.dot(hot, latv[:, at], preferred_element_type=F32)
            lt[:, at] = part
            mean = mean + jnp.sum(part, axis=1, keepdims=True)
        mean = mean / D
        spread = jnp.zeros((C * T, 1), F32)
        for j in range(D // step):
            center = lt[:, j * step : (j + 1) * step] - mean
            spread = spread + jnp.sum(center * center, axis=1, keepdims=True)
        inv = lax.rsqrt(spread / D + 1e-05)
        for j in range(D // step):
            at = slice(j * step, (j + 1) * step)
            nm[:, at] = ((lt[:, at] - mean) * inv * gain_ref[:, at]).astype(BF16)
        for part, weight in ((0, wkv), (1, wvv)):
            pl.when(first)(lambda: locals_[2 + part].wait())
            made = jnp.dot(nm[...], weight[...], preferred_element_type=F32).astype(BF16)
            for c0 in range(C):
                blk = (row * C + c0) * 2 + c
                kv[part, pl.ds(pl.multiple_of(blk * T, T), T), :] = made[c0 * T : (c0 + 1) * T]
                shared(part, blk).start()

        @pl.when(first)
        def _():
            locals_[4].wait()
            own = pl.ds(pl.multiple_of(col * T, T), T)
            qs[...] = jnp.dot(nm[own, :], wqv[...], preferred_element_type=F32).astype(BF16)
            agg_ref[...] = lt[own, pl.ds(pl.multiple_of(s * share, share), share)].astype(BF16)

    ms[...] = jnp.full(ms.shape, -1e30, F32)
    ls[...] = jnp.zeros(ls.shape, F32)
    acc[...] = jnp.zeros(acc.shape, F32)
    scale = 1.0 / math.sqrt(HEAD_DIM)

    def attend(row):
        keys_at = pl.ds(pl.multiple_of(row * W, W), W)
        for h in range(H):
            cols = slice(h * HEAD_DIM, (h + 1) * HEAD_DIM)
            logits = (
                lax.dot_general(
                    qs[:, cols], kv[0, keys_at, cols], (((1,), (1,)), ((), ())),
                    preferred_element_type=F32,
                )
                * scale
            )
            old = ms[h]
            fresh = jnp.maximum(old, jnp.max(logits, axis=1, keepdims=True))
            shrink = jnp.exp(old - fresh)
            expo = jnp.exp(logits - fresh[:, 0:1])
            ls[h] = ls[h] * shrink + jnp.sum(expo, axis=1, keepdims=True)
            ms[h] = fresh
            acc[:, cols] = acc[:, cols] * shrink[:, 0:1] + jnp.dot(
                expo.astype(BF16), kv[1, keys_at, cols], preferred_element_type=F32
            )

    def finish(row):
        for c0 in range(C):
            for part in range(2):
                shared(part, (row * C + c0) * 2 + 1 - c).wait_recv()
        attend(row)

    def turn(i, before):
        dist, way = (i + 1) // 2, lax.rem(i, 2)
        row = r + (1 - 2 * way) * dist
        real = (row >= 0) & (row < R)

        @pl.when(real)
        def _():
            compute(row, i == 0)
            pl.when(i > 0)(lambda: finish(before))

        return jnp.where(real, row, before)

    finish(lax.fori_loop(0, 2 * R - 1, turn, r))

    for h in range(H):
        cols = slice(h * HEAD_DIM, (h + 1) * HEAD_DIM)
        ho[s, :, cols] = (acc[:, cols] / ls[h][:, 0:1]).astype(BF16)
    h_out = [remote(ho.at[s], ho.at[s], h_s.at[k], h_r.at[k], seg_at(k), b) for k in range(1, S)]
    for one in h_out:
        one.start()
    op_out = []
    for k in range(1, S):
        src = seg_at(S - k)
        block = woa.at[src, wo_rows(c)]
        remote(block, block, o_s.at[k], o_r.at[k], s, partner).wait_recv()
        one = remote(block, block, op_s.at[k], op_r.at[k], s, partner)
        one.start()
        op_out.append(one)
    locals_[5].wait()
    lt[0:T, 0:share] = jnp.dot(ho[s], woa[s], preferred_element_type=F32)
    for k in range(1, S):
        src = seg_at(S - k)
        block = woa.at[src, wo_rows(1 - c)]
        remote(block, block, op_s.at[k], op_r.at[k], s, partner).wait_recv()
        remote(ho.at[src], ho.at[src], h_s.at[k], h_r.at[k], s, partner).wait_recv()
        lt[0:T, 0:share] = lt[0:T, 0:share] + jnp.dot(ho[src], woa[src], preferred_element_type=F32)
    att_ref[...] = lt[0:T, 0:share].astype(BF16)

    for one in e_out + ep_out + c_out + o_out + op_out + h_out:
        one.wait_send()

    all_chips(lambda copy: copy.wait_send())

    def drain(i, carry):
        shared(0, i * 2 + c).wait_send()
        shared(1, i * 2 + c).wait_send()
        return carry

    lax.fori_loop(0, chips, drain, 0)


def solution(mesh):
    S = mesh.shape["segment"]
    B = mesh.shape["blk"]
    chips = B // 2
    C = 1
    while C * C * 4 <= chips:
        C *= 2
    R = chips // C

    def on_device(
        pixels, var_group, var_embed, group_weight, agg_query, lat_index, lat_table, norm_gain,
        w_query, w_key, w_value, w_out,
    ):
        vl, D = var_embed.shape
        G, PX, _ = group_weight.shape
        T = pixels.shape[2]
        NL = lat_table.shape[0]
        cl = w_query.shape[1]
        H = cl // HEAD_DIM
        share = D // S
        kp = ((S * vl + G * PX + 8 + 127) // 128) * 128
        vm = pl.BlockSpec(memory_space=pltpu.VMEM)
        far = pl.BlockSpec(memory_space=pltpu.HBM)
        dma = pltpu.SemaphoreType.DMA
        out = jax.ShapeDtypeStruct((T, share), BF16)
        return pl.pallas_call(
            functools.partial(kernel, S, R, C),
            out_shape=(out, out),
            in_specs=[far] * 12,
            out_specs=(vm, vm),
            scratch_shapes=[
                pltpu.VMEM((vl, PX, T), BF16),
                pltpu.VMEM((1, vl), jnp.int32),
                pltpu.VMEM((G, PX, D), BF16),
                pltpu.VMEM((1, D), F32),
                pltpu.VMEM((1, T), jnp.int32),
                pltpu.VMEM((1, D), F32),
                pltpu.VMEM((kp, D), BF16),
                pltpu.VMEM((NL, D), BF16),
                pltpu.VMEM((D, cl), BF16),
                pltpu.VMEM((D, cl), BF16),
                pltpu.VMEM((D, cl), BF16),
                pltpu.VMEM((S, cl, share), BF16),
                pltpu.VMEM((G * PX, D), F32),
                pltpu.VMEM((vl * PX, T), F32),
                pltpu.VMEM((S, vl + G * PX + 16, T), F32),
                pltpu.VMEM((chips, kp, T), F32),
                pltpu.VMEM((C * T, D), F32),
                pltpu.VMEM((C * T, D), BF16),
                pltpu.VMEM((2, B * T, cl), BF16),
                pltpu.VMEM((T, cl), BF16),
                pltpu.VMEM((H, T, 128), F32),
                pltpu.VMEM((H, T, 128), F32),
                pltpu.VMEM((T, cl), F32),
                pltpu.VMEM((S, T, cl), BF16),
                dma((12,)),
            ]
            + [dma((S,))] * 12
            + [dma((chips,)), dma((chips,)), dma((2, B)), dma((2, B))],
            compiler_params=pltpu.CompilerParams(
                collective_id=0, has_side_effects=True, vmem_limit_bytes=67_043_328
            ),
        )(
            pixels,
            var_group.reshape(1, vl),
            var_embed,
            group_weight,
            agg_query.astype(F32).reshape(1, D),
            lat_index.reshape(1, T),
            lat_table,
            norm_gain.reshape(1, D),
            w_query,
            w_key,
            w_value,
            w_out,
        )

    in_specs = (
        P("segment", None, "blk"), P("segment"), P("segment", None), P(), P(), P("blk"), P(), P(),
        P(None, "segment"), P(None, "segment"), P(None, "segment"), P("segment", None),
    )
    out_specs = (P("blk", "segment"), P("blk", "segment"))
    return jax.shard_map(
        on_device, mesh=mesh, in_specs=in_specs, out_specs=out_specs, check_vma=False
    )
```
